32 devices in a mesh: groups: 2 (over x), paths: 2 (over core), feats: 8 (over z, y).
Axes of the slice: x: 2, y: 2, z: 4, core: 2. Of those that a mesh axis runs over, the one named last changes fastest.
Arguments:
- factors: int32 [4096, 128], P(('groups', 'paths')), parts along dimension 0, may hold values from -8 to 8
- frequency: int32 [128, 65536], P(None, 'feats'), may hold values from -48 to 48
- phases: int32 [65536], P('feats'), may hold values from 0 to 1023
- amplitude: float32 [65536], P('feats'), as said below
- targets: float32 [32, 4096], P(None, ('groups', 'paths')), parts along dimension 1, may hold values from -6 to 6
- coeffs_init: float32 [32, 131072], P(None, ('groups', 'feats')), parts along dimension 1, may hold values from -6 to 6
Outputs:
- coeffs: float32 [32, 131072], P(None, ('groups', 'feats')), parts along dimension 1
- predicted: float32 [32, 4096], P(None, ('groups', 'paths')), parts along dimension 1
The draws below stay inside these ranges and needn't reach their ends.
There are 2 independent parts, one for each index of `groups`. The reference program is written for one: setup_inputs(seed, part) draws one part's arguments, and reference() takes and returns one part's arrays. A program takes and returns all parts, laid end to end along the dimension named above; an argument that names none is the same for every part. Nothing has to cross between parts.
Inputs may be any that keep to these rules, and one draw needn't show every extreme that they name: `amplitude`: positive feature weights.
All inputs are finite; a program needn't handle non-finite values.
Results may differ from the reference program's by a relative error of at most 0.00026.
Values sent between devices are 32-bit elements; how exact they have to be, the bound alone decides.
A program may use at most 128 MiB of HBM per device.

```python
import math
import jax
import jax.numpy as jnp
from jax import lax

F = 65536
K = 128
V = 32
ITERS = 3
PATHS = 2048


def draw_amplitude(key, part):
    index = jnp.arange(F, dtype=jnp.float32)
    rising = jnp.exp(jnp.log(3.0) * index / F)
    spread = jnp.exp(jax.random.uniform(key, (F,), jnp.float32, minval=-1.2, maxval=1.2))
    return (spread * rising * jnp.sqrt(1.0 / F)).astype(jnp.float32)


def place_ends(array, key, smallest, top_value):
    longest = array.shape.index(max(array.shape))
    spots = []
    for shift in (0, 1):
        where = [jax.random.randint(jax.random.fold_in(key, axis), (), 0, length) for axis, length in enumerate(array.shape)]
        where[longest] = (where[longest] + shift) % array.shape[longest]
        spots.append(tuple(where))
    return array.at[spots[0]].set(smallest).at[spots[1]].set(top_value)


def block_scale(own_key, shape, cuts, low, high):
    loudness, own = 1.0, jax.random.fold_in(own_key, 6)
    for position, shards_of in cuts:
        steps = jnp.exp(jax.random.uniform(jax.random.fold_in(own, position), (shards_of,), jnp.float32, low / len(cuts), high / len(cuts)))
        loudness = loudness * jnp.repeat(steps, shape[position] // shards_of).reshape([-1 if axis == position else 1 for axis in range(len(shape))])
    return loudness


def bell_draw(own_key, dims, scale, bound, pieces=(), held_as=jnp.bfloat16):
    level = block_scale(own_key, dims, pieces, -0.22, 0.18) if pieces else 1.0
    values = jax.random.normal(own_key, dims, jnp.float32) * scale * level
    return jnp.minimum(jnp.maximum(values, -bound), bound).astype(held_as)


def setup_inputs(seed: int = 0, part: int = 0) -> dict:
    streams_of = jax.random.split(jax.random.key(seed), 7)
    part_keys = jax.random.split(jax.random.fold_in(streams_of[6], part), 7)
    factors = place_ends(jax.random.randint(part_keys[0], (PATHS, K), -8, 9), jax.random.fold_in(part_keys[0], 1), -8, 8).astype(jnp.int32)
    frequency = place_ends(jax.random.randint(streams_of[1], (K, F), 0 - 6144 // K, 6144 // K + 1), jax.random.fold_in(streams_of[1], 1), 0 - 6144 // K, (6144 // K + 1) - 1).astype(jnp.int32)
    phases = place_ends(jax.random.randint(streams_of[2], (F,), 0, 1024), jax.random.fold_in(streams_of[2], 1), 0, 1023).astype(jnp.int32)
    amplitude = draw_amplitude(jax.random.fold_in(streams_of[6], 71), part)
    targets = bell_draw(part_keys[4], (V, PATHS), 1.0, 6.0, ((1, 2),), jnp.float32)
    coeffs_init = bell_draw(part_keys[5], (V, F), 1.0, 6.0, ((1, 8),), jnp.float32)
    return {"factors": factors, "frequency": frequency, "phases": phases, "amplitude": amplitude, "targets": targets, "coeffs_init": coeffs_init}


huber_cap = 1.0
step_rate = 0.2
momentum = 0.9
epsilon = 1e-06

def build(factor_vals, freq_block, phase_block, amp_block):
    summed = jnp.dot(factor_vals, freq_block, precision=lax.Precision.HIGHEST, preferred_element_type=jnp.float32)
    return amp_block * jnp.cos(summed * 0.0025 + phase_block * (2.0 * math.pi / 1024.0))

def reference(factors, frequency, phases, amplitude, targets, coeffs_init):
    block_cols = min(F, 2048)
    nblocks = F // block_cols
    total_paths = targets.shape[1]
    factor_vals = factors.astype(jnp.float32)
    freq_blocks = jnp.transpose(frequency.astype(jnp.float32).reshape(K, nblocks, block_cols), (1, 0, 2))
    phase_blocks = phases.astype(jnp.float32).reshape(nblocks, block_cols)
    amp_blocks = amplitude.reshape(nblocks, block_cols)

    def feature_block(index):
        return build(factor_vals, freq_blocks[index], phase_blocks[index], amp_blocks[index])

    def predict(coeffs):
        coeff_blocks = jnp.transpose(coeffs.reshape(V, nblocks, block_cols), (1, 0, 2))

        def step(total, index):
            block = feature_block(index)
            part = lax.dot_general(coeff_blocks[index], block, (((1,), (1,)), ((), ())), precision=lax.Precision.HIGHEST, preferred_element_type=jnp.float32)
            return (total + part, None)
        total, _ = lax.scan(step, jnp.zeros((V, total_paths), jnp.float32), jnp.arange(nblocks, dtype=jnp.int32))
        return total
    coeffs = coeffs_init
    velocity = jnp.zeros_like(coeffs_init)
    predicted = predict(coeffs)
    for turn in range(ITERS):
        clipped = jnp.clip(predicted - targets, -huber_cap, huber_cap)

        def grad_step(carry, index):
            block = feature_block(index)
            return (carry, jnp.dot(clipped, block, precision=lax.Precision.HIGHEST, preferred_element_type=jnp.float32))
        _, grad_blocks = lax.scan(grad_step, jnp.float32(0.0), jnp.arange(nblocks, dtype=jnp.int32))
        gradient = jnp.transpose(grad_blocks, (1, 0, 2)).reshape(V, F)
        scale = jnp.sqrt(jnp.mean(gradient * gradient) + epsilon)
        velocity = momentum * velocity + gradient / scale
        coeffs = coeffs - step_rate * velocity
        predicted = predict(coeffs)
    return (coeffs, predicted)
```

```python
import functools
import math

import jax
import jax.numpy as jnp
from jax import lax
from jax.experimental import pallas as pl
from jax.experimental.pallas import tpu as pltpu
from jax.sharding import PartitionSpec as P

huber_cap = 1.0
step_rate = 0.2
momentum = 0.9
epsilon = 1e-06
ITERS = 3
BF = jnp.bfloat16
F8 = jnp.float8_e4m3fn
F32 = jnp.float32
MESH = pl.DeviceIdType.MESH
NT = (((1,), (1,)), ((), ()))

TURN = 0.0025 / (2.0 * math.pi)
C0, C1, C2, C3 = -0.7991282213187093, 3.943309301080472, -3.236024302046346, -0.3193029597879815
COS_GAIN = 3.131803039470962
LO_GAIN = 2.0**17
CLIP_GAIN = 256.0
INIT_GAIN = 64.0
DIGIT = 16.0


def cos_turns(t):
    r = t - jnp.round(t)
    u = r * r
    y = ((u + C2) * u + C1) * u + C0
    return y * y + C3


def split(x):
    hi = x.astype(BF)
    return hi, (x - hi.astype(F32)).astype(BF)


def digits(x):
    first = x.astype(F8)
    return first, ((x - first.astype(F32)) * DIGIT).astype(F8)


def kernel(
    fac_ref, freq_ref, phase_ref, amp_ref, target_ref, init_ref, coef_ref, pred_ref,
    fac, hi, lo, gain, rel, mine, pair, grad, velocity, ys, y8, xs, x8, image, pieces, state, track, out, sent,
    sq_mine, sq_all,
    pair_send, pair_recv, rs_send, rs_recv, ag_send, ag_recv, sq_send, sq_recv,
    *, n, tile, count, bound,
):
    chunks, v, chunk = image.shape
    feats = mine.shape[1]
    team = n // chunks
    core = lax.axis_index("paths")
    me = lax.axis_index("feats")
    other = 1 - core
    own = me // team
    rank = lax.rem(me, team)
    if chunks == 4:
        order = [3 - own, lax.rem(own + 2, 4), own + 1 - 2 * lax.rem(own, 2), own]
    else:
        order = [lax.rem(own + 1 + i, chunks) for i in range(chunks)]

    barrier = pltpu.get_barrier_semaphore()
    pl.semaphore_signal(barrier, inc=1, device_id={"paths": other}, device_id_type=MESH)
    for d in range(1, n):
        pl.semaphore_signal(barrier, inc=1, device_id={"feats": lax.rem(me + d, n)}, device_id_type=MESH)

    def columns(j, size):
        return pl.ds(pl.multiple_of(j * size, size), size)

    def pair_copy(slot, j):
        at = columns(j, tile)
        return pltpu.make_async_remote_copy(
            mine.at[:, at], pair.at[slot, :, at], pair_send.at[j], pair_recv.at[slot, j],
            device_id={"paths": other}, device_id_type=MESH)

    def rs_copy(slot, c, j, s):
        return pltpu.make_async_remote_copy(
            image.at[c], pieces.at[slot, s], rs_send.at[j], rs_recv.at[slot, s],
            device_id={"feats": j}, device_id_type=MESH)

    def ag_copy(c, s):
        return pltpu.make_async_remote_copy(
            out, sent.at[s], ag_send.at[c], ag_recv.at[s],
            device_id={"feats": c * team + rank}, device_id_type=MESH)

    def sq_copy(slot, j, s):
        return pltpu.make_async_remote_copy(
            sq_mine, sq_all.at[slot, s], sq_send.at[j], sq_recv.at[slot, s],
            device_id={"feats": j}, device_id_type=MESH)

    amp = amp_ref[...]
    top = jnp.max(amp, axis=1, keepdims=True)
    gain[...] = amp * COS_GAIN
    rel[...] = amp / top
    fac[...] = fac_ref[...].astype(F32).astype(BF)
    coef_ref[...] = init_ref[...]
    velocity[...] = jnp.zeros_like(velocity)
    track[...] = jnp.zeros_like(track)

    btile = min(512, feats)

    def build(j, carry):
        at = columns(j, btile)
        freq = freq_ref[:, at].astype(F32).astype(BF)
        phase = phase_ref[:, at].astype(F32) * (1.0 / 1024.0)
        summed = jnp.dot(fac[...], freq, preferred_element_type=F32)
        c = cos_turns(summed * TURN + phase)
        h = c.astype(BF)
        hi[:, at] = h
        lo[:, at] = ((c - h.astype(F32)) * LO_GAIN).astype(F8)
        w = init_ref[:, at]
        ys[:v, at], ys[v:, at] = split(w * gain[:, at])
        y8[:v, at], y8[v:, at] = digits(w * rel[:, at] * INIT_GAIN)
        return carry

    lax.fori_loop(0, feats // btile, build, 0)
    pl.semaphore_wait(barrier, n)

    def push(slot, lo_scale):
        for i, c in enumerate(order):
            at = columns(c, chunk)
            big = lax.dot_general(ys[...], hi[at, :], NT, preferred_element_type=F32)
            small = lax.dot_general(y8[...], lo[at, :], NT, preferred_element_type=F32)
            value = big[:v] + big[v:] + (small[:v] + small[v:] * (1.0 / DIGIT)) * lo_scale
            if i == chunks - 1:
                pieces[slot, me] = value
            image[c] = value
            for e in range(team):
                j = c * team + e
                if i < chunks - 1:
                    rs_copy(slot, c, j, me).start()
                else:

                    @pl.when(j != me)
                    def _():
                        rs_copy(slot, c, j, me).start()

    def reduced(slot):
        for d in range(1, n):
            s = lax.rem(me + d, n)
            rs_copy(slot, own, s, s).wait_recv()
        total = pieces[slot, 0]
        for s in range(1, n):
            total = total + pieces[slot, s]
        return total

    def spread(value):
        out[...] = value
        for c in order[:-1]:
            ag_copy(c, own).start()
        sent[own] = value

    def settle(slot):
        for c in order[:-1]:
            ag_copy(c, own).wait_send()
        for d in range(1, n):
            rs_copy(slot, own, lax.rem(me + d, n), me).wait_send()

    target = columns(own, chunk)
    push(0, top * (COS_GAIN / (INIT_GAIN * LO_GAIN)))
    start = reduced(0)
    state[...] = start
    spread(jnp.clip(start - target_ref[:, target], -huber_cap, huber_cap))
    settle(0)
    tiles = feats // tile

    def turn(it, carry):
        slot = lax.rem(it, 2)
        after = 1 - slot

        for i, c in enumerate(order[::-1]):
            if i > 0:
                ag_copy(c, c).wait_recv()
            x = sent[c]
            xs[:v, :], xs[v:, :] = split(x)
            x8[:v, :], x8[v:, :] = digits(x * CLIP_GAIN)
            down = columns(c, chunk)

            def pull(j, carry):
                at = columns(j, tile)
                big = jnp.dot(xs[...], hi[down, at], preferred_element_type=F32)
                small = jnp.dot(x8[...], lo[down, at], preferred_element_type=F32)
                value = big[:v] + big[v:] + (small[:v] + small[v:] * (1.0 / DIGIT)) * (1.0 / (CLIP_GAIN * LO_GAIN))
                mine[:, at] = value if i == 0 else mine[:, at] + value
                if i == chunks - 1:
                    pair_copy(slot, j).start()
                return carry

            lax.fori_loop(0, tiles, pull, 0)

        def join(j, squares):
            at = columns(j, tile)
            pair_copy(slot, j).wait()
            u = mine[:, at] + pair[slot, :, at]
            g = u * gain[:, at]
            grad[:, at] = g
            ys[:v, at], ys[v:, at] = split(g * gain[:, at])
            r = rel[:, at]
            y8[:v, at], y8[v:, at] = digits(u * (r * r) * bound)
            square = g * g
            fold = sum(square[k : k + 8] for k in range(0, v, 8))
            return squares + sum(fold[:, k : k + 128] for k in range(0, tile, 128))

        squares = lax.fori_loop(0, tiles, join, jnp.zeros((8, 128), F32))
        sq_mine[...] = squares
        for d in range(1, n):
            sq_copy(slot, lax.rem(me + d, n), me).start()
        sq_all[slot, me] = squares

        push(after, top * top * (COS_GAIN * COS_GAIN / (bound * LO_GAIN)))

        for d in range(1, n):
            s = lax.rem(me + d, n)
            sq_copy(slot, s, s).wait_recv()
        squares = jnp.sum(sq_all[slot], axis=0)
        squares = jnp.sum(jnp.sum(squares, axis=0, keepdims=True), axis=1, keepdims=True)
        scale = jnp.sqrt(squares / count + epsilon)

        moved = momentum * track[...] + reduced(after) / scale
        track[...] = moved
        predicted = state[...] - step_rate * moved
        state[...] = predicted
        clipped = jnp.clip(predicted - target_ref[:, target], -huber_cap, huber_cap)
        spread(jnp.where(it == ITERS - 1, predicted, clipped))

        def advance(j, carry):
            at = columns(j, tile)
            vel = momentum * velocity[:, at] + grad[:, at] / scale
            velocity[:, at] = vel
            coef_ref[:, at] = coef_ref[:, at] - step_rate * vel
            return carry

        lax.fori_loop(0, tiles, advance, 0)
        for d in range(1, n):
            sq_copy(slot, lax.rem(me + d, n), me).wait_send()
        settle(after)
        return carry

    lax.fori_loop(0, ITERS, turn, 0)
    for c in order[:-1]:
        ag_copy(c, c).wait_recv()
    for c in range(chunks):
        pred_ref[:, c * chunk : (c + 1) * chunk] = sent[c]


def fit(factors, frequency, phases, amplitude, targets, coeffs, n, total, paths_total):
    cols, k = factors.shape
    v, feats = coeffs.shape
    chunks = min(max(cols // 256, 1), n)
    chunk = cols // chunks
    tile = min(1024, feats)
    tiles = feats // tile
    vm = pl.BlockSpec(memory_space=pltpu.VMEM)
    dma = pltpu.SemaphoreType.DMA
    return pl.pallas_call(
        functools.partial(kernel, n=n, tile=tile, count=float(v * total), bound=200.0 / paths_total),
        in_specs=[vm] * 6,
        out_specs=[vm, vm],
        out_shape=[jax.ShapeDtypeStruct((v, feats), F32), jax.ShapeDtypeStruct((v, cols), F32)],
        scratch_shapes=[
            pltpu.VMEM((cols, k), BF),
            pltpu.VMEM((cols, feats), BF),
            pltpu.VMEM((cols, feats), F8),
            pltpu.VMEM((1, feats), F32),
            pltpu.VMEM((1, feats), F32),
            pltpu.VMEM((v, feats), F32),
            pltpu.VMEM((2, v, feats), F32),
            pltpu.VMEM((v, feats), F32),
            pltpu.VMEM((v, feats), F32),
            pltpu.VMEM((2 * v, feats), BF),
            pltpu.VMEM((2 * v, feats), F8),
            pltpu.VMEM((2 * v, chunk), BF),
            pltpu.VMEM((2 * v, chunk), F8),
            pltpu.VMEM((chunks, v, chunk), F32),
            pltpu.VMEM((2, n, v, chunk), F32),
            pltpu.VMEM((v, chunk), F32),
            pltpu.VMEM((v, chunk), F32),
            pltpu.VMEM((v, chunk), F32),
            pltpu.VMEM((chunks, v, chunk), F32),
            pltpu.VMEM((8, 128), F32),
            pltpu.VMEM((2, n, 8, 128), F32),
            dma((tiles,)), dma((2, tiles)),
            dma((n,)), dma((2, n)), dma((chunks,)), dma((chunks,)), dma((n,)), dma((2, n)),
        ],
        compiler_params=pltpu.CompilerParams(
            collective_id=0, has_side_effects=True, vmem_limit_bytes=56 << 20),
        name="fit",
    )(factors, frequency, phases, amplitude, targets, coeffs)


def solution(mesh):
    n = mesh.shape["feats"]

    def body(factors, frequency, phases, amplitude, targets, coeffs_init):
        total = frequency.shape[1] * n
        paths_total = factors.shape[0] * mesh.shape["paths"]
        return fit(factors, frequency, phases[None, :], amplitude[None, :], targets, coeffs_init, n, total, paths_total)

    return jax.shard_map(
        body,
        mesh=mesh,
        in_specs=(
            P(("groups", "paths"), None),
            P(None, "feats"),
            P("feats"),
            P("feats"),
            P(None, ("groups", "paths")),
            P(None, ("groups", "feats")),
        ),
        out_specs=(P(None, ("groups", "feats")), P(None, ("groups", "paths"))),
        check_vma=False,
    )
```

```python
import functools
import math

import jax
import jax.numpy as jnp
from jax import lax
from jax.experimental import pallas as pl
from jax.experimental.pallas import tpu as pltpu
from jax.sharding import PartitionSpec as P

huber_cap = 1.0
step_rate = 0.2
momentum = 0.9
epsilon = 1e-06
ITERS = 3
BF = jnp.bfloat16
F8 = jnp.float8_e4m3fn
F32 = jnp.float32
MESH = pl.DeviceIdType.MESH
NT = (((1,), (1,)), ((), ()))

TURN = 0.0025 / (2.0 * math.pi)
C0, C1, C2, C3 = -0.7991282213187093, 3.943309301080472, -3.236024302046346, -0.3193029597879815
COS_GAIN = 3.131803039470962
LO_GAIN = 2.0**17
CLIP_GAIN = 256.0
INIT_GAIN = 64.0
DIGIT = 16.0


def cos_turns(t):
    r = t - jnp.round(t)
    u = r * r
    y = ((u + C2) * u + C1) * u + C0
    return y * y + C3


def split(x):
    hi = x.astype(BF)
    return hi, (x - hi.astype(F32)).astype(BF)


def digits(x):
    first = x.astype(F8)
    return first, ((x - first.astype(F32)) * DIGIT).astype(F8)


def joined(small, v):
    return small[:v] + small[v:] * (1.0 / DIGIT)


def kernel(
    fac_ref, freq_ref, phase_ref, amp_ref, target_ref, init_ref, coef_ref, pred_ref,
    fac, hi, turned, lo, gain, rel, mine, pair, grad, velocity, ys, y8, xs, x8, image, pieces, state, track, out, sent,
    sq_mine, sq_all,
    pair_send, pair_recv, rs_send, rs_recv, ag_send, ag_recv, sq_send, sq_recv,
    *, n, per_row, rows, width, chunk, tile, count, bound,
):
    v, cols = image.shape
    feats = mine.shape[1]
    per_chunk = chunk // width
    chunks = cols // chunk
    groups = n // per_row
    core = lax.axis_index("paths")
    me = lax.axis_index("feats")
    other = 1 - core

    barrier = pltpu.get_barrier_semaphore()
    pl.semaphore_signal(barrier, inc=1, device_id={"paths": other}, device_id_type=MESH)
    for d in range(1, n):
        pl.semaphore_signal(barrier, inc=1, device_id={"feats": lax.rem(me + d, n)}, device_id_type=MESH)

    def spot(j):
        r = pl.ds(pl.multiple_of((j // per_row) * rows, rows), rows)
        c = pl.ds(pl.multiple_of(lax.rem(j, per_row) * width, width), width)
        return r, c

    def columns(j, size):
        return pl.ds(pl.multiple_of(j * size, size), size)

    def pair_copy(slot, j, size):
        at = columns(j, size)
        return pltpu.make_async_remote_copy(
            mine.at[:, at], pair.at[slot, :, at], pair_send.at[j], pair_recv.at[slot, j],
            device_id={"paths": other}, device_id_type=MESH)

    def rs_copy(j):
        return pltpu.make_async_remote_copy(
            image.at[spot(j)], pieces.at[me], rs_send.at[j], rs_recv.at[me],
            device_id={"feats": j}, device_id_type=MESH)

    def rs_arrival(s):
        return pltpu.make_async_remote_copy(
            image.at[spot(me)], pieces.at[s], rs_send.at[s], rs_recv.at[s],
            device_id={"feats": s}, device_id_type=MESH)

    def ag_copy(j):
        return pltpu.make_async_remote_copy(
            out, sent.at[spot(me)], ag_send.at[j], ag_recv.at[me],
            device_id={"feats": j}, device_id_type=MESH)

    def ag_arrival(s):
        return pltpu.make_async_remote_copy(
            out, sent.at[spot(s)], ag_send.at[s], ag_recv.at[s],
            device_id={"feats": s}, device_id_type=MESH)

    def sq_copy(j):
        return pltpu.make_async_remote_copy(
            sq_mine, sq_all.at[me], sq_send.at[j], sq_recv.at[me],
            device_id={"feats": j}, device_id_type=MESH)

    def sq_arrival(s):
        return pltpu.make_async_remote_copy(
            sq_mine, sq_all.at[s], sq_send.at[s], sq_recv.at[s],
            device_id={"feats": s}, device_id_type=MESH)

    amp = amp_ref[...]
    top = jnp.max(amp, axis=1, keepdims=True)
    gain[...] = amp * COS_GAIN
    rel[...] = amp / top
    fac[...] = fac_ref[...].astype(F32).astype(BF)
    coef_ref[...] = init_ref[...]
    velocity[...] = jnp.zeros_like(velocity)
    track[...] = jnp.zeros_like(track)

    btile = min(512, feats)

    def build(j, carry):
        at = columns(j, btile)
        freq = freq_ref[:, at].astype(F32).astype(BF)
        phase = phase_ref[:, at].astype(F32) * (1.0 / 1024.0)
        summed = jnp.dot(fac[...], freq, preferred_element_type=F32)
        c = cos_turns(summed * TURN + phase)
        h = c.astype(BF)
        hi[:, at] = h
        turned[at, :] = h.T
        lo[:, at] = ((c - h.astype(F32)) * LO_GAIN).astype(F8)
        w = init_ref[:, at]
        ys[:v, at], ys[v:, at] = split(w * gain[:, at])
        y8[:v, at], y8[v:, at] = digits(w * rel[:, at] * INIT_GAIN)
        return carry

    lax.fori_loop(0, feats // btile, build, 0)
    pl.semaphore_wait(barrier, n)

    def push(lo_scale):
        own = lax.rem(me, per_row) // per_chunk
        if chunks == 4:
            order = [3 - own, lax.rem(own + 2, 4), own + 1 - 2 * lax.rem(own, 2), own]
        else:
            order = [lax.rem(own + 1 + i, chunks) for i in range(chunks)]
        for c in order:
            at = columns(c, chunk)
            big = jnp.dot(ys[...], turned[:, at], preferred_element_type=F32)
            small = lax.dot_general(y8[...], lo[at, :], NT, preferred_element_type=F32)
            image[:, at] = big[:v] + big[v:] + joined(small, v) * lo_scale
            for g in range(groups):
                for e in range(per_chunk):
                    j = g * per_row + c * per_chunk + e

                    @pl.when(j != me)
                    def _():
                        rs_copy(j).start()

    def reduced():
        total = image[spot(me)]
        for d in range(1, n):
            s = lax.rem(me + d, n)
            rs_arrival(s).wait_recv()
            total = total + pieces[s]
        return total

    def spread(value):
        out[...] = value
        for d in range(1, n):
            ag_copy(lax.rem(me + d, n)).start()
        sent[spot(me)] = value

    def gathered():
        for d in range(1, n):
            ag_arrival(lax.rem(me + d, n)).wait_recv()
        for d in range(1, n):
            j = lax.rem(me + d, n)
            rs_copy(j).wait_send()
            ag_copy(j).wait_send()

    push(top * (COS_GAIN / (INIT_GAIN * LO_GAIN)))
    start = reduced()
    state[...] = start
    spread(jnp.clip(start - target_ref[spot(me)], -huber_cap, huber_cap))
    gathered()

    top_gain = bound
    pieces_of = feats // tile

    def turn(it, carry):
        slot = lax.rem(it, 2)
        x = sent[...]
        xs[:v, :], xs[v:, :] = split(x)
        x8[:v, :], x8[v:, :] = digits(x * CLIP_GAIN)

        def pull(j, carry):
            at = columns(j, tile)
            big = jnp.dot(xs[...], hi[:, at], preferred_element_type=F32)
            small = jnp.dot(x8[...], lo[:, at], preferred_element_type=F32)
            mine[:, at] = big[:v] + big[v:] + joined(small, v) * (1.0 / (CLIP_GAIN * LO_GAIN))
            pair_copy(slot, j, tile).start()
            return carry

        lax.fori_loop(0, pieces_of, pull, 0)

        def join(j, squares):
            at = columns(j, tile)
            pair_copy(slot, j, tile).wait()
            u = mine[:, at] + pair[slot, :, at]
            g = u * gain[:, at]
            grad[:, at] = g
            ys[:v, at], ys[v:, at] = split(g * gain[:, at])
            r = rel[:, at]
            y8[:v, at], y8[v:, at] = digits(u * (r * r) * top_gain)
            square = g * g
            fold = sum(square[k : k + 8] for k in range(0, v, 8))
            return squares + sum(fold[:, k : k + 128] for k in range(0, tile, 128))

        squares = lax.fori_loop(0, pieces_of, join, jnp.zeros((8, 128), F32))
        sq_mine[...] = squares
        for d in range(1, n):
            sq_copy(lax.rem(me + d, n)).start()
        sq_all[me] = squares

        push(top * top * (COS_GAIN * COS_GAIN / (top_gain * LO_GAIN)))

        for d in range(1, n):
            sq_arrival(lax.rem(me + d, n)).wait_recv()
        squares = jnp.sum(sq_all[...], axis=0)
        squares = jnp.sum(jnp.sum(squares, axis=0, keepdims=True), axis=1, keepdims=True)
        scale = jnp.sqrt(squares / count + epsilon)

        moved = momentum * track[...] + reduced() / scale
        track[...] = moved
        predicted = state[...] - step_rate * moved
        state[...] = predicted
        clipped = jnp.clip(predicted - target_ref[spot(me)], -huber_cap, huber_cap)
        spread(jnp.where(it == ITERS - 1, predicted, clipped))

        def advance(j, carry):
            at = columns(j, tile)
            vel = momentum * velocity[:, at] + grad[:, at] / scale
            velocity[:, at] = vel
            coef_ref[:, at] = coef_ref[:, at] - step_rate * vel
            return carry

        lax.fori_loop(0, pieces_of, advance, 0)
        for d in range(1, n):
            sq_copy(lax.rem(me + d, n)).wait_send()
        gathered()
        return carry

    lax.fori_loop(0, ITERS, turn, 0)
    pred_ref[...] = sent[...]


def fit(factors, frequency, phases, amplitude, targets, coeffs, n, total, paths_total):
    cols, k = factors.shape
    v, feats = coeffs.shape
    per_row = min(n, cols // 128)
    width = cols // per_row
    rows = v // (n // per_row)
    chunk = max(width, min(256, cols))
    tile = min(1024, feats)
    pieces_of = feats // tile
    vm = pl.BlockSpec(memory_space=pltpu.VMEM)
    dma = pltpu.SemaphoreType.DMA
    return pl.pallas_call(
        functools.partial(
            kernel, n=n, per_row=per_row, rows=rows, width=width, chunk=chunk, tile=tile,
            count=float(v * total), bound=200.0 / paths_total),
        in_specs=[vm] * 6,
        out_specs=[vm, vm],
        out_shape=[jax.ShapeDtypeStruct((v, feats), F32), jax.ShapeDtypeStruct((v, cols), F32)],
        scratch_shapes=[
            pltpu.VMEM((cols, k), BF),
            pltpu.VMEM((cols, feats), BF),
            pltpu.VMEM((feats, cols), BF),
            pltpu.VMEM((cols, feats), F8),
            pltpu.VMEM((1, feats), F32),
            pltpu.VMEM((1, feats), F32),
            pltpu.VMEM((v, feats), F32),
            pltpu.VMEM((2, v, feats), F32),
            pltpu.VMEM((v, feats), F32),
            pltpu.VMEM((v, feats), F32),
            pltpu.VMEM((2 * v, feats), BF),
            pltpu.VMEM((2 * v, feats), F8),
            pltpu.VMEM((2 * v, cols), BF),
            pltpu.VMEM((2 * v, cols), F8),
            pltpu.VMEM((v, cols), F32),
            pltpu.VMEM((n, rows, width), F32),
            pltpu.VMEM((rows, width), F32),
            pltpu.VMEM((rows, width), F32),
            pltpu.VMEM((rows, width), F32),
            pltpu.VMEM((v, cols), F32),
            pltpu.VMEM((8, 128), F32),
            pltpu.VMEM((n, 8, 128), F32),
            dma((pieces_of,)), dma((2, pieces_of)),
            dma((n,)), dma((n,)), dma((n,)), dma((n,)), dma((n,)), dma((n,)),
        ],
        compiler_params=pltpu.CompilerParams(
            collective_id=0, has_side_effects=True, vmem_limit_bytes=60 << 20),
        name="fit",
    )(factors, frequency, phases, amplitude, targets, coeffs)


def solution(mesh):
    n = mesh.shape["feats"]

    def body(factors, frequency, phases, amplitude, targets, coeffs_init):
        total = frequency.shape[1] * n
        paths_total = factors.shape[0] * mesh.shape["paths"]
        return fit(factors, frequency, phases[None, :], amplitude[None, :], targets, coeffs_init, n, total, paths_total)

    return jax.shard_map(
        body,
        mesh=mesh,
        in_specs=(
            P(("groups", "paths"), None),
            P(None, "feats"),
            P("feats"),
            P("feats"),
            P(None, ("groups", "paths")),
            P(None, ("groups", "feats")),
        ),
        out_specs=(P(None, ("groups", "feats")), P(None, ("groups", "paths"))),
        check_vma=False,
    )
```

```python
import functools
import math

import jax
import jax.numpy as jnp
from jax import lax
from jax.experimental import pallas as pl
from jax.experimental.pallas import tpu as pltpu
from jax.sharding import PartitionSpec as P

huber_cap = 1.0
step_rate = 0.2
momentum = 0.9
epsilon = 1e-06
ITERS = 3
BF = jnp.bfloat16
F8 = jnp.float8_e4m3fn
F32 = jnp.float32
MESH = pl.DeviceIdType.MESH
NT = (((1,), (1,)), ((), ()))

TURN = 0.0025 / (2.0 * math.pi)
C0, C1, C2, C3 = -0.7991282213187093, 3.943309301080472, -3.236024302046346, -0.3193029597879815
COS_GAIN = 3.131803039470962
LO_GAIN = 2.0**17
CLIP_GAIN = 256.0
INIT_GAIN = 64.0
DIGIT = 16.0


def cos_turns(t):
    r = t - jnp.round(t)
    u = r * r
    y = ((u + C2) * u + C1) * u + C0
    return y * y + C3


def split(x):
    hi = x.astype(BF)
    return hi, (x - hi.astype(F32)).astype(BF)


def digits(x):
    first = x.astype(F8)
    return first, ((x - first.astype(F32)) * DIGIT).astype(F8)


def joined(small, v):
    return small[:v] + small[v:] * (1.0 / DIGIT)


def kernel(
    fac_ref, freq_ref, phase_ref, amp_ref, target_ref, init_ref, coef_out, pred_ref,
    freq_buf, coef, fac, hi, turned, lo, gain, rel, mine, pair, grad, velocity, ys, y8, xs, x8, image, pieces, state, track, out, sent,
    sq_mine, sq_all,
    pair_send, pair_recv, rs_send, rs_recv, ag_send, ag_recv, sq_send, sq_recv, freq_sem, init_sem, coef_sem,
    *, n, per_row, rows, width, chunk, tile, count, bound,
):
    v, cols = image.shape
    feats = mine.shape[1]
    per_chunk = chunk // width
    chunks = cols // chunk
    groups = n // per_row
    core = lax.axis_index("paths")
    me = lax.axis_index("feats")
    other = 1 - core

    btile = min(512, feats)
    loads = feats // btile

    def load_copies(j):
        at = pl.ds(pl.multiple_of(j * btile, btile), btile)
        return (
            pltpu.make_async_copy(freq_ref.at[:, at], freq_buf.at[:, at], freq_sem.at[j]),
            pltpu.make_async_copy(init_ref.at[:, at], coef.at[:, at], init_sem.at[j]))

    for j in range(loads):
        for copy in load_copies(j):
            copy.start()

    barrier = pltpu.get_barrier_semaphore()
    pl.semaphore_signal(barrier, inc=1, device_id={"paths": other}, device_id_type=MESH)
    for d in range(1, n):
        pl.semaphore_signal(barrier, inc=1, device_id={"feats": lax.rem(me + d, n)}, device_id_type=MESH)

    def spot(j):
        r = pl.ds(pl.multiple_of((j // per_row) * rows, rows), rows)
        c = pl.ds(pl.multiple_of(lax.rem(j, per_row) * width, width), width)
        return r, c

    def columns(j, size):
        return pl.ds(pl.multiple_of(j * size, size), size)

    def pair_copy(slot, j, size):
        at = columns(j, size)
        return pltpu.make_async_remote_copy(
            mine.at[:, at], pair.at[slot, :, at], pair_send.at[j], pair_recv.at[slot, j],
            device_id={"paths": other}, device_id_type=MESH)

    def rs_copy(j):
        return pltpu.make_async_remote_copy(
            image.at[spot(j)], pieces.at[me], rs_send.at[j], rs_recv.at[me],
            device_id={"feats": j}, device_id_type=MESH)

    def rs_arrival(s):
        return pltpu.make_async_remote_copy(
            image.at[spot(me)], pieces.at[s], rs_send.at[s], rs_recv.at[s],
            device_id={"feats": s}, device_id_type=MESH)

    def ag_copy(j):
        return pltpu.make_async_remote_copy(
            out, sent.at[spot(me)], ag_send.at[j], ag_recv.at[me],
            device_id={"feats": j}, device_id_type=MESH)

    def ag_arrival(s):
        return pltpu.make_async_remote_copy(
            out, sent.at[spot(s)], ag_send.at[s], ag_recv.at[s],
            device_id={"feats": s}, device_id_type=MESH)

    def sq_copy(j):
        return pltpu.make_async_remote_copy(
            sq_mine, sq_all.at[me], sq_send.at[j], sq_recv.at[me],
            device_id={"feats": j}, device_id_type=MESH)

    def sq_arrival(s):
        return pltpu.make_async_remote_copy(
            sq_mine, sq_all.at[s], sq_send.at[s], sq_recv.at[s],
            device_id={"feats": s}, device_id_type=MESH)

    amp = amp_ref[...]
    top = jnp.max(amp, axis=1, keepdims=True)
    gain[...] = amp * COS_GAIN
    rel[...] = amp / top
    fac[...] = fac_ref[...].astype(F32).astype(BF)
    velocity[...] = jnp.zeros_like(velocity)
    track[...] = jnp.zeros_like(track)

    def build(j, carry):
        at = columns(j, btile)
        for copy in load_copies(j):
            copy.wait()
        freq = freq_buf[:, at].astype(F32).astype(BF)
        phase = phase_ref[:, at].astype(F32) * (1.0 / 1024.0)
        summed = jnp.dot(fac[...], freq, preferred_element_type=F32)
        c = cos_turns(summed * TURN + phase)
        h = c.astype(BF)
        hi[:, at] = h
        turned[at, :] = h.T
        lo[:, at] = ((c - h.astype(F32)) * LO_GAIN).astype(F8)
        w = coef[:, at]
        ys[:v, at], ys[v:, at] = split(w * gain[:, at])
        y8[:v, at], y8[v:, at] = digits(w * rel[:, at] * INIT_GAIN)
        return carry

    lax.fori_loop(0, loads, build, 0)
    pl.semaphore_wait(barrier, n)

    def push(lo_scale):
        own = lax.rem(me, per_row) // per_chunk
        if chunks == 4:
            order = [3 - own, lax.rem(own + 2, 4), own + 1 - 2 * lax.rem(own, 2), own]
        else:
            order = [lax.rem(own + 1 + i, chunks) for i in range(chunks)]
        for c in order:
            at = columns(c, chunk)
            big = jnp.dot(ys[...], turned[:, at], preferred_element_type=F32)
            small = lax.dot_general(y8[...], lo[at, :], NT, preferred_element_type=F32)
            image[:, at] = big[:v] + big[v:] + joined(small, v) * lo_scale
            for g in range(groups):
                for e in range(per_chunk):
                    j = g * per_row + c * per_chunk + e

                    @pl.when(j != me)
                    def _():
                        rs_copy(j).start()

    def reduced():
        total = image[spot(me)]
        for d in range(1, n):
            s = lax.rem(me + d, n)
            rs_arrival(s).wait_recv()
            total = total + pieces[s]
        return total

    def spread(value):
        out[...] = value
        for d in range(1, n):
            ag_copy(lax.rem(me + d, n)).start()
        sent[spot(me)] = value

    def gathered():
        for d in range(1, n):
            ag_arrival(lax.rem(me + d, n)).wait_recv()
        for d in range(1, n):
            j = lax.rem(me + d, n)
            rs_copy(j).wait_send()
            ag_copy(j).wait_send()

    push(top * (COS_GAIN / (INIT_GAIN * LO_GAIN)))
    start = reduced()
    state[...] = start
    spread(jnp.clip(start - target_ref[spot(me)], -huber_cap, huber_cap))
    gathered()

    coef_copy = pltpu.make_async_copy(coef, coef_out, coef_sem)
    top_gain = bound
    pieces_of = feats // tile

    def turn(it, carry):
        slot = lax.rem(it, 2)
        x = sent[...]
        xs[:v, :], xs[v:, :] = split(x)
        x8[:v, :], x8[v:, :] = digits(x * CLIP_GAIN)

        def pull(j, carry):
            at = columns(j, tile)
            big = jnp.dot(xs[...], hi[:, at], preferred_element_type=F32)
            small = jnp.dot(x8[...], lo[:, at], preferred_element_type=F32)
            mine[:, at] = big[:v] + big[v:] + joined(small, v) * (1.0 / (CLIP_GAIN * LO_GAIN))
            pair_copy(slot, j, tile).start()
            return carry

        lax.fori_loop(0, pieces_of, pull, 0)

        def join(j, squares):
            at = columns(j, tile)
            pair_copy(slot, j, tile).wait()
            u = mine[:, at] + pair[slot, :, at]
            g = u * gain[:, at]
            grad[:, at] = g
            ys[:v, at], ys[v:, at] = split(g * gain[:, at])
            r = rel[:, at]
            y8[:v, at], y8[v:, at] = digits(u * (r * r) * top_gain)
            square = g * g
            fold = sum(square[k : k + 8] for k in range(0, v, 8))
            return squares + sum(fold[:, k : k + 128] for k in range(0, tile, 128))

        squares = lax.fori_loop(0, pieces_of, join, jnp.zeros((8, 128), F32))
        sq_mine[...] = squares
        for d in range(1, n):
            sq_copy(lax.rem(me + d, n)).start()
        sq_all[me] = squares

        push(top * top * (COS_GAIN * COS_GAIN / (top_gain * LO_GAIN)))

        for d in range(1, n):
            sq_arrival(lax.rem(me + d, n)).wait_recv()
        squares = jnp.sum(sq_all[...], axis=0)
        squares = jnp.sum(jnp.sum(squares, axis=0, keepdims=True), axis=1, keepdims=True)
        scale = jnp.sqrt(squares / count + epsilon)

        moved = momentum * track[...] + reduced() / scale
        track[...] = moved
        predicted = state[...] - step_rate * moved
        state[...] = predicted
        clipped = jnp.clip(predicted - target_ref[spot(me)], -huber_cap, huber_cap)
        spread(jnp.where(it == ITERS - 1, predicted, clipped))

        def advance(j, carry):
            at = columns(j, tile)
            vel = momentum * velocity[:, at] + grad[:, at] / scale
            velocity[:, at] = vel
            coef[:, at] = coef[:, at] - step_rate * vel
            return carry

        lax.fori_loop(0, pieces_of, advance, 0)
        for d in range(1, n):
            sq_copy(lax.rem(me + d, n)).wait_send()

        @pl.when(it == ITERS - 1)
        def _():
            coef_copy.start()

        gathered()
        return carry

    lax.fori_loop(0, ITERS, turn, 0)
    pred_ref[...] = sent[...]
    coef_copy.wait()


def result_kernel(coef_ref, pred_ref, coef_out, pred_out, coef, pred, in_sem, out_sem):
    steps = [(pred_ref, pred, pred_out)]
    for r in range(0, coef.shape[0], 8):
        steps.append((coef_ref.at[r : r + 8], coef.at[r : r + 8], coef_out.at[r : r + 8]))
    loads = [pltpu.make_async_copy(a, b, in_sem.at[i]) for i, (a, b, _) in enumerate(steps)]
    stores = [pltpu.make_async_copy(b, c, out_sem.at[i]) for i, (_, b, c) in enumerate(steps)]
    for load in loads:
        load.start()
    for load, store in zip(loads, stores):
        load.wait()
        store.start()
    for store in stores:
        store.wait()


def results(coeffs, predicted):
    anywhere = pl.BlockSpec(memory_space=pl.ANY)
    steps = 1 + coeffs.shape[0] // 8
    return pl.pallas_call(
        result_kernel,
        in_specs=[anywhere, anywhere],
        out_specs=[anywhere, anywhere],
        out_shape=[jax.ShapeDtypeStruct(x.shape, x.dtype) for x in (coeffs, predicted)],
        scratch_shapes=[
            pltpu.VMEM(coeffs.shape, F32),
            pltpu.VMEM(predicted.shape, F32),
            pltpu.SemaphoreType.DMA((steps,)),
            pltpu.SemaphoreType.DMA((steps,)),
        ],
        name="results",
    )(coeffs, predicted)


def fit(factors, frequency, phases, amplitude, targets, coeffs, n, total, paths_total):
    cols, k = factors.shape
    v, feats = coeffs.shape
    per_row = min(n, cols // 128)
    width = cols // per_row
    rows = v // (n // per_row)
    chunk = max(width, min(256, cols))
    tile = min(1024, feats)
    pieces_of = feats // tile
    vm = pl.BlockSpec(memory_space=pltpu.VMEM)
    anywhere = pl.BlockSpec(memory_space=pl.ANY)
    loads = feats // min(512, feats)
    dma = pltpu.SemaphoreType.DMA
    return pl.pallas_call(
        functools.partial(
            kernel, n=n, per_row=per_row, rows=rows, width=width, chunk=chunk, tile=tile,
            count=float(v * total), bound=200.0 / paths_total),
        in_specs=[vm, anywhere, vm, vm, vm, anywhere],
        out_specs=[anywhere, vm],
        out_shape=[jax.ShapeDtypeStruct((v, feats), F32), jax.ShapeDtypeStruct((v, cols), F32)],
        scratch_shapes=[
            pltpu.VMEM((k, feats), jnp.int32),
            pltpu.VMEM((v, feats), F32),
            pltpu.VMEM((cols, k), BF),
            pltpu.VMEM((cols, feats), BF),
            pltpu.VMEM((feats, cols), BF),
            pltpu.VMEM((cols, feats), F8),
            pltpu.VMEM((1, feats), F32),
            pltpu.VMEM((1, feats), F32),
            pltpu.VMEM((v, feats), F32),
            pltpu.VMEM((2, v, feats), F32),
            pltpu.VMEM((v, feats), F32),
            pltpu.VMEM((v, feats), F32),
            pltpu.VMEM((2 * v, feats), BF),
            pltpu.VMEM((2 * v, feats), F8),
            pltpu.VMEM((2 * v, cols), BF),
            pltpu.VMEM((2 * v, cols), F8),
            pltpu.VMEM((v, cols), F32),
            pltpu.VMEM((n, rows, width), F32),
            pltpu.VMEM((rows, width), F32),
            pltpu.VMEM((rows, width), F32),
            pltpu.VMEM((rows, width), F32),
            pltpu.VMEM((v, cols), F32),
            pltpu.VMEM((8, 128), F32),
            pltpu.VMEM((n, 8, 128), F32),
            dma((pieces_of,)), dma((2, pieces_of)),
            dma((n,)), dma((n,)), dma((n,)), dma((n,)), dma((n,)), dma((n,)),
            dma((loads,)), dma((loads,)), dma,
        ],
        compiler_params=pltpu.CompilerParams(
            collective_id=0, has_side_effects=True, vmem_limit_bytes=60 << 20),
        name="fit",
    )(factors, frequency, phases, amplitude, targets, coeffs)


def solution(mesh):
    n = mesh.shape["feats"]

    def body(factors, frequency, phases, amplitude, targets, coeffs_init):
        total = frequency.shape[1] * n
        paths_total = factors.shape[0] * mesh.shape["paths"]
        return results(*fit(
            factors, frequency, phases[None, :], amplitude[None, :], targets, coeffs_init, n, total, paths_total))

    return jax.shard_map(
        body,
        mesh=mesh,
        in_specs=(
            P(("groups", "paths"), None),
            P(None, "feats"),
            P("feats"),
            P("feats"),
            P(None, ("groups", "paths")),
            P(None, ("groups", "feats")),
        ),
        out_specs=(P(None, ("groups", "feats")), P(None, ("groups", "paths"))),
        check_vma=False,
    )
```

```python
import functools
import math

import jax
import jax.numpy as jnp
from jax import lax
from jax.experimental import pallas as pl
from jax.experimental.pallas import tpu as pltpu
from jax.sharding import PartitionSpec as P

huber_cap = 1.0
step_rate = 0.2
momentum = 0.9
epsilon = 1e-06
ITERS = 3
BF = jnp.bfloat16
F8 = jnp.float8_e4m3fn
F32 = jnp.float32
MESH = pl.DeviceIdType.MESH
NT = (((1,), (1,)), ((), ()))

TURN = 0.0025 / (2.0 * math.pi)
C0, C1, C2, C3 = -0.7991282213187093, 3.943309301080472, -3.236024302046346, -0.3193029597879815
COS_GAIN = 3.131803039470962
LO_GAIN = 2.0**17
CLIP_GAIN = 256.0
INIT_GAIN = 64.0
DIGIT = 16.0


def cos_turns(t):
    r = t - jnp.round(t)
    u = r * r
    y = ((u + C2) * u + C1) * u + C0
    return y * y + C3


def split(x):
    hi = x.astype(BF)
    return hi, (x - hi.astype(F32)).astype(BF)


def digits(x):
    first = x.astype(F8)
    return first, ((x - first.astype(F32)) * DIGIT).astype(F8)


def joined(small, v):
    return small[:v] + small[v:] * (1.0 / DIGIT)


def kernel(
    fac_ref, freq_ref, phase_ref, amp_ref, target_ref, init_ref, coef_out, pred_ref,
    freq_buf, coef, fac, hi, turned, lo, gain, rel, mine, pair, grad, velocity, ys, y8, xs, x8, image, pieces, state, track, out, sent,
    sq_mine, sq_all,
    pair_send, pair_recv, rs_send, rs_recv, ag_send, ag_recv, sq_send, sq_recv, freq_sem, init_sem, coef_sem,
    *, n, per_row, rows, width, chunk, tile, count, bound,
):
    v, cols = image.shape
    feats = mine.shape[1]
    per_chunk = chunk // width
    chunks = cols // chunk
    groups = n // per_row
    core = lax.axis_index("paths")
    me = lax.axis_index("feats")
    other = 1 - core

    btile = min(1024, feats)
    loads = feats // btile

    def load_copies(j):
        at = pl.ds(pl.multiple_of(j * btile, btile), btile)
        return (
            pltpu.make_async_copy(freq_ref.at[:, at], freq_buf.at[:, at], freq_sem.at[j]),
            pltpu.make_async_copy(init_ref.at[:, at], coef.at[:, at], init_sem.at[j]))

    for j in range(loads):
        for copy in load_copies(j):
            copy.start()

    barrier = pltpu.get_barrier_semaphore()
    pl.semaphore_signal(barrier, inc=1, device_id={"paths": other}, device_id_type=MESH)
    for d in range(1, n):
        pl.semaphore_signal(barrier, inc=1, device_id={"feats": lax.rem(me + d, n)}, device_id_type=MESH)

    def spot(j):
        r = pl.ds(pl.multiple_of((j // per_row) * rows, rows), rows)
        c = pl.ds(pl.multiple_of(lax.rem(j, per_row) * width, width), width)
        return r, c

    def columns(j, size):
        return pl.ds(pl.multiple_of(j * size, size), size)

    def pair_copy(slot, j, size):
        at = columns(j, size)
        return pltpu.make_async_remote_copy(
            mine.at[:, at], pair.at[slot, :, at], pair_send.at[j], pair_recv.at[slot, j],
            device_id={"paths": other}, device_id_type=MESH)

    def rs_copy(j):
        return pltpu.make_async_remote_copy(
            image.at[spot(j)], pieces.at[me], rs_send.at[j], rs_recv.at[me],
            device_id={"feats": j}, device_id_type=MESH)

    def rs_arrival(s):
        return pltpu.make_async_remote_copy(
            image.at[spot(me)], pieces.at[s], rs_send.at[s], rs_recv.at[s],
            device_id={"feats": s}, device_id_type=MESH)

    def ag_copy(j):
        return pltpu.make_async_remote_copy(
            out, sent.at[spot(me)], ag_send.at[j], ag_recv.at[me],
            device_id={"feats": j}, device_id_type=MESH)

    def ag_arrival(s):
        return pltpu.make_async_remote_copy(
            out, sent.at[spot(s)], ag_send.at[s], ag_recv.at[s],
            device_id={"feats": s}, device_id_type=MESH)

    def sq_copy(j):
        return pltpu.make_async_remote_copy(
            sq_mine, sq_all.at[me], sq_send.at[j], sq_recv.at[me],
            device_id={"feats": j}, device_id_type=MESH)

    def sq_arrival(s):
        return pltpu.make_async_remote_copy(
            sq_mine, sq_all.at[s], sq_send.at[s], sq_recv.at[s],
            device_id={"feats": s}, device_id_type=MESH)

    amp = amp_ref[...]
    top = jnp.max(amp, axis=1, keepdims=True)
    gain[...] = amp * COS_GAIN
    rel[...] = amp / top
    fac[...] = fac_ref[...].astype(F32).astype(BF)
    velocity[...] = jnp.zeros_like(velocity)
    track[...] = jnp.zeros_like(track)

    def build(j, carry):
        at = columns(j, btile)
        for copy in load_copies(j):
            copy.wait()
        freq = freq_buf[:, at].astype(F32).astype(BF)
        phase = phase_ref[:, at].astype(F32) * (1.0 / 1024.0)
        summed = jnp.dot(fac[...], freq, preferred_element_type=F32)
        c = cos_turns(summed * TURN + phase)
        h = c.astype(BF)
        hi[:, at] = h
        turned[at, :] = h.T
        lo[:, at] = ((c - h.astype(F32)) * LO_GAIN).astype(F8)
        w = coef[:, at]
        ys[:v, at], ys[v:, at] = split(w * gain[:, at])
        y8[:v, at], y8[v:, at] = digits(w * rel[:, at] * INIT_GAIN)
        return carry

    lax.fori_loop(0, loads, build, 0)
    pl.semaphore_wait(barrier, n)

    def push(lo_scale):
        own = lax.rem(me, per_row) // per_chunk
        if chunks == 4:
            order = [3 - own, lax.rem(own + 2, 4), own + 1 - 2 * lax.rem(own, 2), own]
        else:
            order = [lax.rem(own + 1 + i, chunks) for i in range(chunks)]
        for c in order:
            at = columns(c, chunk)
            big = jnp.dot(ys[...], turned[:, at], preferred_element_type=F32)
            small = lax.dot_general(y8[...], lo[at, :], NT, preferred_element_type=F32)
            image[:, at] = big[:v] + big[v:] + joined(small, v) * lo_scale
            for g in range(groups):
                for e in range(per_chunk):
                    j = g * per_row + c * per_chunk + e

                    @pl.when(j != me)
                    def _():
                        rs_copy(j).start()

    def reduced():
        total = image[spot(me)]
        for d in range(1, n):
            s = lax.rem(me + d, n)
            rs_arrival(s).wait_recv()
            total = total + pieces[s]
        return total

    def mirrored(d):
        if n & (n - 1):
            return lax.rem(me + d, n)
        j, bit = me, 1
        while bit < n:
            if d & bit:
                j = j + bit - 2 * bit * lax.rem(me // bit, 2)
            bit *= 2
        return j

    def spread(value):
        out[...] = value
        for d in range(n - 1, 0, -1):
            ag_copy(mirrored(d)).start()
        sent[spot(me)] = value

    def gathered():
        for d in range(1, n):
            rs_copy(lax.rem(me + d, n)).wait_send()
        for d in range(1, n):
            ag_arrival(mirrored(d)).wait_recv()

    def all_spread():
        for d in range(1, n):
            ag_copy(lax.rem(me + d, n)).wait_send()

    push(top * (COS_GAIN / (INIT_GAIN * LO_GAIN)))
    start = reduced()
    state[...] = start
    spread(jnp.clip(start - target_ref[spot(me)], -huber_cap, huber_cap))
    gathered()

    coef_copy = pltpu.make_async_copy(coef, coef_out, coef_sem)
    top_gain = bound
    pieces_of = feats // tile

    def turn(it, carry):
        slot = lax.rem(it, 2)
        x = sent[...]
        xs[:v, :], xs[v:, :] = split(x)
        x8[:v, :], x8[v:, :] = digits(x * CLIP_GAIN)

        def pull(j, carry):
            at = columns(j, tile)
            big = jnp.dot(xs[...], hi[:, at], preferred_element_type=F32)
            small = jnp.dot(x8[...], lo[:, at], preferred_element_type=F32)
            mine[:, at] = big[:v] + big[v:] + joined(small, v) * (1.0 / (CLIP_GAIN * LO_GAIN))
            pair_copy(slot, j, tile).start()
            return carry

        lax.fori_loop(0, pieces_of, pull, 0)

        def join(j, squares):
            at = columns(j, tile)
            pair_copy(slot, j, tile).wait()
            u = mine[:, at] + pair[slot, :, at]
            g = u * gain[:, at]
            grad[:, at] = g
            ys[:v, at], ys[v:, at] = split(g * gain[:, at])
            r = rel[:, at]
            y8[:v, at], y8[v:, at] = digits(u * (r * r) * top_gain)
            square = g * g
            fold = sum(square[k : k + 8] for k in range(0, v, 8))
            return squares + sum(fold[:, k : k + 128] for k in range(0, tile, 128))

        squares = lax.fori_loop(0, pieces_of, join, jnp.zeros((8, 128), F32))
        sq_mine[...] = squares
        for d in range(1, n):
            sq_copy(lax.rem(me + d, n)).start()
        sq_all[me] = squares

        push(top * top * (COS_GAIN * COS_GAIN / (top_gain * LO_GAIN)))

        all_spread()
        for d in range(1, n):
            sq_arrival(lax.rem(me + d, n)).wait_recv()
        squares = jnp.sum(sq_all[...], axis=0)
        squares = jnp.sum(jnp.sum(squares, axis=0, keepdims=True), axis=1, keepdims=True)
        scale = jnp.sqrt(squares / count + epsilon)

        moved = momentum * track[...] + reduced() / scale
        track[...] = moved
        predicted = state[...] - step_rate * moved
        state[...] = predicted
        clipped = jnp.clip(predicted - target_ref[spot(me)], -huber_cap, huber_cap)
        spread(jnp.where(it == ITERS - 1, predicted, clipped))

        def advance(j, carry):
            at = columns(j, tile)
            vel = momentum * velocity[:, at] + grad[:, at] / scale
            velocity[:, at] = vel
            coef[:, at] = coef[:, at] - step_rate * vel
            return carry

        lax.fori_loop(0, pieces_of, advance, 0)
        for d in range(1, n):
            sq_copy(lax.rem(me + d, n)).wait_send()

        @pl.when(it == ITERS - 1)
        def _():
            coef_copy.start()

        gathered()
        return carry

    lax.fori_loop(0, ITERS, turn, 0)
    pred_ref[...] = sent[...]
    all_spread()
    coef_copy.wait()


def result_kernel(coef_ref, pred_ref, coef_out, pred_out, coef, pred, in_sem, out_sem):
    steps = [(pred_ref, pred, pred_out)]
    for r in range(0, coef.shape[0], 8):
        steps.append((coef_ref.at[r : r + 8], coef.at[r : r + 8], coef_out.at[r : r + 8]))
    loads = [pltpu.make_async_copy(a, b, in_sem.at[i]) for i, (a, b, _) in enumerate(steps)]
    stores = [pltpu.make_async_copy(b, c, out_sem.at[i]) for i, (_, b, c) in enumerate(steps)]
    for load in loads:
        load.start()
    for load, store in zip(loads, stores):
        load.wait()
        store.start()
    for store in stores:
        store.wait()


def results(coeffs, predicted):
    anywhere = pl.BlockSpec(memory_space=pl.ANY)
    steps = 1 + coeffs.shape[0] // 8
    return pl.pallas_call(
        result_kernel,
        in_specs=[anywhere, anywhere],
        out_specs=[anywhere, anywhere],
        out_shape=[jax.ShapeDtypeStruct(x.shape, x.dtype) for x in (coeffs, predicted)],
        scratch_shapes=[
            pltpu.VMEM(coeffs.shape, F32),
            pltpu.VMEM(predicted.shape, F32),
            pltpu.SemaphoreType.DMA((steps,)),
            pltpu.SemaphoreType.DMA((steps,)),
        ],
        name="results",
    )(coeffs, predicted)


def fit(factors, frequency, phases, amplitude, targets, coeffs, n, total, paths_total):
    cols, k = factors.shape
    v, feats = coeffs.shape
    per_row = min(n, cols // 128)
    width = cols // per_row
    rows = v // (n // per_row)
    chunk = max(width, min(256, cols))
    tile = min(2048, feats)
    pieces_of = feats // tile
    vm = pl.BlockSpec(memory_space=pltpu.VMEM)
    anywhere = pl.BlockSpec(memory_space=pl.ANY)
    loads = feats // min(1024, feats)
    dma = pltpu.SemaphoreType.DMA
    return pl.pallas_call(
        functools.partial(
            kernel, n=n, per_row=per_row, rows=rows, width=width, chunk=chunk, tile=tile,
            count=float(v * total), bound=200.0 / paths_total),
        in_specs=[vm, anywhere, vm, vm, vm, anywhere],
        out_specs=[anywhere, vm],
        out_shape=[jax.ShapeDtypeStruct((v, feats), F32), jax.ShapeDtypeStruct((v, cols), F32)],
        scratch_shapes=[
            pltpu.VMEM((k, feats), jnp.int32),
            pltpu.VMEM((v, feats), F32),
            pltpu.VMEM((cols, k), BF),
            pltpu.VMEM((cols, feats), BF),
            pltpu.VMEM((feats, cols), BF),
            pltpu.VMEM((cols, feats), F8),
            pltpu.VMEM((1, feats), F32),
            pltpu.VMEM((1, feats), F32),
            pltpu.VMEM((v, feats), F32),
            pltpu.VMEM((2, v, feats), F32),
            pltpu.VMEM((v, feats), F32),
            pltpu.VMEM((v, feats), F32),
            pltpu.VMEM((2 * v, feats), BF),
            pltpu.VMEM((2 * v, feats), F8),
            pltpu.VMEM((2 * v, cols), BF),
            pltpu.VMEM((2 * v, cols), F8),
            pltpu.VMEM((v, cols), F32),
            pltpu.VMEM((n, rows, width), F32),
            pltpu.VMEM((rows, width), F32),
            pltpu.VMEM((rows, width), F32),
            pltpu.VMEM((rows, width), F32),
            pltpu.VMEM((v, cols), F32),
            pltpu.VMEM((8, 128), F32),
            pltpu.VMEM((n, 8, 128), F32),
            dma((pieces_of,)), dma((2, pieces_of)),
            dma((n,)), dma((n,)), dma((n,)), dma((n,)), dma((n,)), dma((n,)),
            dma((loads,)), dma((loads,)), dma,
        ],
        compiler_params=pltpu.CompilerParams(
            collective_id=0, has_side_effects=True, vmem_limit_bytes=60 << 20),
        name="fit",
    )(factors, frequency, phases, amplitude, targets, coeffs)


def solution(mesh):
    n = mesh.shape["feats"]

    def body(factors, frequency, phases, amplitude, targets, coeffs_init):
        total = frequency.shape[1] * n
        paths_total = factors.shape[0] * mesh.shape["paths"]
        return results(*fit(
            factors, frequency, phases[None, :], amplitude[None, :], targets, coeffs_init, n, total, paths_total))

    return jax.shard_map(
        body,
        mesh=mesh,
        in_specs=(
            P(("groups", "paths"), None),
            P(None, "feats"),
            P("feats"),
            P("feats"),
            P(None, ("groups", "paths")),
            P(None, ("groups", "feats")),
        ),
        out_specs=(P(None, ("groups", "feats")), P(None, ("groups", "paths"))),
        check_vma=False,
    )
```

```python
import functools
import math

import jax
import jax.numpy as jnp
from jax import lax
from jax.experimental import pallas as pl
from jax.experimental.pallas import tpu as pltpu
from jax.sharding import PartitionSpec as P

huber_cap = 1.0
step_rate = 0.2
momentum = 0.9
epsilon = 1e-06
ITERS = 3
BF = jnp.bfloat16
F8 = jnp.float8_e4m3fn
F32 = jnp.float32
MESH = pl.DeviceIdType.MESH
NT = (((1,), (1,)), ((), ()))

TURN = 0.0025 / (2.0 * math.pi)
C0, C1, C2, C3 = -0.7991282213187093, 3.943309301080472, -3.236024302046346, -0.3193029597879815
COS_GAIN = 3.131803039470962
LO_GAIN = 2.0**17
CLIP_GAIN = 256.0
INIT_GAIN = 64.0
DIGIT = 16.0


def cos_turns(t):
    r = t - jnp.round(t)
    u = r * r
    y = ((u + C2) * u + C1) * u + C0
    return y * y + C3


def split(x):
    hi = x.astype(BF)
    return hi, (x - hi.astype(F32)).astype(BF)


def digits(x):
    first = x.astype(F8)
    return first, ((x - first.astype(F32)) * DIGIT).astype(F8)


def joined(small, v):
    return small[:v] + small[v:] * (1.0 / DIGIT)


def kernel(
    fac_ref, freq_ref, phase_ref, amp_ref, target_ref, init_ref, coef_out, pred_ref,
    freq_buf, coef, fac, hi, turned, lo, gain, rel, mine, pair, grad, velocity, ys, y8, xs, x8, image, pieces, state, track, out, sent,
    sq_mine, sq_all,
    pair_send, pair_recv, rs_send, rs_recv, ag_send, ag_recv, sq_send, sq_recv, freq_sem, init_sem, coef_sem,
    *, n, per_row, rows, width, chunk, tile, count, bound,
):
    v, cols = image.shape
    feats = mine.shape[1]
    per_chunk = chunk // width
    chunks = cols // chunk
    groups = n // per_row
    core = lax.axis_index("paths")
    me = lax.axis_index("feats")
    other = 1 - core

    btile = min(1024, feats)
    loads = feats // btile

    def load_copies(j):
        at = pl.ds(pl.multiple_of(j * btile, btile), btile)
        return (
            pltpu.make_async_copy(freq_ref.at[:, at], freq_buf.at[:, at], freq_sem.at[j]),
            pltpu.make_async_copy(init_ref.at[:, at], coef.at[:, at], init_sem.at[j]))

    for j in range(loads):
        for copy in load_copies(j):
            copy.start()

    barrier = pltpu.get_barrier_semaphore()
    pl.semaphore_signal(barrier, inc=1, device_id={"paths": other}, device_id_type=MESH)
    for d in range(1, n):
        pl.semaphore_signal(barrier, inc=1, device_id={"feats": lax.rem(me + d, n)}, device_id_type=MESH)

    def spot(j):
        r = pl.ds(pl.multiple_of((j // per_row) * rows, rows), rows)
        c = pl.ds(pl.multiple_of(lax.rem(j, per_row) * width, width), width)
        return r, c

    def columns(j, size):
        return pl.ds(pl.multiple_of(j * size, size), size)

    def pair_copy(slot, j, size):
        at = columns(j, size)
        return pltpu.make_async_remote_copy(
            mine.at[:, at], pair.at[slot, :, at], pair_send.at[j], pair_recv.at[slot, j],
            device_id={"paths": other}, device_id_type=MESH)

    def rs_copy(j):
        return pltpu.make_async_remote_copy(
            image.at[spot(j)], pieces.at[me], rs_send.at[j], rs_recv.at[me],
            device_id={"feats": j}, device_id_type=MESH)

    def rs_arrival(s):
        return pltpu.make_async_remote_copy(
            image.at[spot(me)], pieces.at[s], rs_send.at[s], rs_recv.at[s],
            device_id={"feats": s}, device_id_type=MESH)

    def ag_copy(j):
        return pltpu.make_async_remote_copy(
            out, sent.at[spot(me)], ag_send.at[j], ag_recv.at[me],
            device_id={"feats": j}, device_id_type=MESH)

    def ag_arrival(s):
        return pltpu.make_async_remote_copy(
            out, sent.at[spot(s)], ag_send.at[s], ag_recv.at[s],
            device_id={"feats": s}, device_id_type=MESH)

    def sq_copy(j):
        return pltpu.make_async_remote_copy(
            sq_mine, sq_all.at[me], sq_send.at[j], sq_recv.at[me],
            device_id={"feats": j}, device_id_type=MESH)

    def sq_arrival(s):
        return pltpu.make_async_remote_copy(
            sq_mine, sq_all.at[s], sq_send.at[s], sq_recv.at[s],
            device_id={"feats": s}, device_id_type=MESH)

    amp = amp_ref[...]
    top = jnp.max(amp, axis=1, keepdims=True)
    gain[...] = amp * COS_GAIN
    rel[...] = amp / top
    fac[...] = fac_ref[...].astype(F32).astype(BF)
    velocity[...] = jnp.zeros_like(velocity)
    track[...] = jnp.zeros_like(track)

    def build(j, carry):
        at = columns(j, btile)
        for copy in load_copies(j):
            copy.wait()
        freq = freq_buf[:, at].astype(F32).astype(BF)
        phase = phase_ref[:, at].astype(F32) * (1.0 / 1024.0)
        summed = jnp.dot(fac[...], freq, preferred_element_type=F32)
        c = cos_turns(summed * TURN + phase)
        h = c.astype(BF)
        hi[:, at] = h
        turned[at, :] = h.T
        lo[:, at] = ((c - h.astype(F32)) * LO_GAIN).astype(F8)
        w = coef[:, at]
        ys[:v, at], ys[v:, at] = split(w * gain[:, at])
        y8[:v, at], y8[v:, at] = digits(w * rel[:, at] * INIT_GAIN)
        return carry

    lax.fori_loop(0, loads, build, 0)
    pl.semaphore_wait(barrier, n)

    def push(lo_scale):
        own = lax.rem(me, per_row) // per_chunk
        if chunks == 4:
            order = [3 - own, lax.rem(own + 2, 4), own + 1 - 2 * lax.rem(own, 2), own]
        else:
            order = [lax.rem(own + 1 + i, chunks) for i in range(chunks)]
        for c in order:
            at = columns(c, chunk)
            big = jnp.dot(ys[...], turned[:, at], preferred_element_type=F32)
            small = lax.dot_general(y8[...], lo[at, :], NT, preferred_element_type=F32)
            image[:, at] = big[:v] + big[v:] + joined(small, v) * lo_scale
            for g in range(groups):
                for e in range(per_chunk):
                    j = g * per_row + c * per_chunk + e

                    @pl.when(j != me)
                    def _():
                        rs_copy(j).start()

    def reduced():
        total = image[spot(me)]
        for d in range(1, n):
            s = lax.rem(me + d, n)
            rs_arrival(s).wait_recv()
            total = total + pieces[s]
        return total

    def mirrored(d):
        if n & (n - 1):
            return lax.rem(me + d, n)
        j, bit = me, 1
        while bit < n:
            if d & bit:
                j = j + bit - 2 * bit * lax.rem(me // bit, 2)
            bit *= 2
        return j

    def spread(value):
        out[...] = value
        for d in range(n - 1, 0, -1):
            ag_copy(mirrored(d)).start()
        sent[spot(me)] = value

    halves = per_row // 2
    side = lax.rem(me, per_row) // halves
    near, far = columns(side, cols // 2), columns(1 - side, cols // 2)

    def settled():
        for d in range(1, n):
            rs_copy(lax.rem(me + d, n)).wait_send()

    def gathered(late):
        for d in range(1, n):
            if late == bool(d & halves and not n & (n - 1)):
                ag_arrival(mirrored(d)).wait_recv()

    def all_spread():
        for d in range(1, n):
            ag_copy(lax.rem(me + d, n)).wait_send()

    push(top * (COS_GAIN / (INIT_GAIN * LO_GAIN)))
    start = reduced()
    state[...] = start
    spread(jnp.clip(start - target_ref[spot(me)], -huber_cap, huber_cap))
    settled()

    coef_copy = pltpu.make_async_copy(coef, coef_out, coef_sem)
    top_gain = bound
    pieces_of = feats // tile

    def turn(it, carry):
        slot = lax.rem(it, 2)
        def arrange(part):
            x = sent[:, part]
            xs[:v, part], xs[v:, part] = split(x)
            x8[:v, part], x8[v:, part] = digits(x * CLIP_GAIN)

        def pulled(part, at):
            big = jnp.dot(xs[:, part], hi[part, at], preferred_element_type=F32)
            small = jnp.dot(x8[:, part], lo[part, at], preferred_element_type=F32)
            return big[:v] + big[v:] + joined(small, v) * (1.0 / (CLIP_GAIN * LO_GAIN))

        gathered(False)
        arrange(near)
        for j in range(pieces_of):
            at = columns(j, tile)
            mine[:, at] = pulled(near, at)
        gathered(True)
        arrange(far)
        for j in range(pieces_of):
            at = columns(j, tile)
            mine[:, at] = mine[:, at] + pulled(far, at)
            pair_copy(slot, j, tile).start()

        def join(j, squares):
            at = columns(j, tile)
            pair_copy(slot, j, tile).wait()
            u = mine[:, at] + pair[slot, :, at]
            g = u * gain[:, at]
            grad[:, at] = g
            ys[:v, at], ys[v:, at] = split(g * gain[:, at])
            r = rel[:, at]
            y8[:v, at], y8[v:, at] = digits(u * (r * r) * top_gain)
            square = g * g
            fold = sum(square[k : k + 8] for k in range(0, v, 8))
            return squares + sum(fold[:, k : k + 128] for k in range(0, tile, 128))

        squares = lax.fori_loop(0, pieces_of, join, jnp.zeros((8, 128), F32))
        sq_mine[...] = squares
        for d in range(1, n):
            sq_copy(lax.rem(me + d, n)).start()
        sq_all[me] = squares

        push(top * top * (COS_GAIN * COS_GAIN / (top_gain * LO_GAIN)))

        all_spread()
        for d in range(1, n):
            sq_arrival(lax.rem(me + d, n)).wait_recv()
        squares = jnp.sum(sq_all[...], axis=0)
        squares = jnp.sum(jnp.sum(squares, axis=0, keepdims=True), axis=1, keepdims=True)
        scale = jnp.sqrt(squares / count + epsilon)

        moved = momentum * track[...] + reduced() / scale
        track[...] = moved
        predicted = state[...] - step_rate * moved
        state[...] = predicted
        clipped = jnp.clip(predicted - target_ref[spot(me)], -huber_cap, huber_cap)
        spread(jnp.where(it == ITERS - 1, predicted, clipped))

        def advance(j, carry):
            at = columns(j, tile)
            vel = momentum * velocity[:, at] + grad[:, at] / scale
            velocity[:, at] = vel
            coef[:, at] = coef[:, at] - step_rate * vel
            return carry

        lax.fori_loop(0, pieces_of, advance, 0)
        for d in range(1, n):
            sq_copy(lax.rem(me + d, n)).wait_send()

        @pl.when(it == ITERS - 1)
        def _():
            coef_copy.start()

        settled()
        return carry

    lax.fori_loop(0, ITERS, turn, 0)
    gathered(False)
    gathered(True)
    pred_ref[...] = sent[...]
    all_spread()
    coef_copy.wait()


def result_kernel(coef_ref, pred_ref, coef_out, pred_out, coef, pred, in_sem, out_sem):
    steps = [(pred_ref, pred, pred_out)]
    for r in range(0, coef.shape[0], 8):
        steps.append((coef_ref.at[r : r + 8], coef.at[r : r + 8], coef_out.at[r : r + 8]))
    loads = [pltpu.make_async_copy(a, b, in_sem.at[i]) for i, (a, b, _) in enumerate(steps)]
    stores = [pltpu.make_async_copy(b, c, out_sem.at[i]) for i, (_, b, c) in enumerate(steps)]
    for load in loads:
        load.start()
    for load, store in zip(loads, stores):
        load.wait()
        store.start()
    for store in stores:
        store.wait()


def results(coeffs, predicted):
    anywhere = pl.BlockSpec(memory_space=pl.ANY)
    steps = 1 + coeffs.shape[0] // 8
    return pl.pallas_call(
        result_kernel,
        in_specs=[anywhere, anywhere],
        out_specs=[anywhere, anywhere],
        out_shape=[jax.ShapeDtypeStruct(x.shape, x.dtype) for x in (coeffs, predicted)],
        scratch_shapes=[
            pltpu.VMEM(coeffs.shape, F32),
            pltpu.VMEM(predicted.shape, F32),
            pltpu.SemaphoreType.DMA((steps,)),
            pltpu.SemaphoreType.DMA((steps,)),
        ],
        name="results",
    )(coeffs, predicted)


def fit(factors, frequency, phases, amplitude, targets, coeffs, n, total, paths_total):
    cols, k = factors.shape
    v, feats = coeffs.shape
    per_row = min(n, cols // 128)
    width = cols // per_row
    rows = v // (n // per_row)
    chunk = max(width, min(256, cols))
    tile = min(2048, feats)
    pieces_of = feats // tile
    vm = pl.BlockSpec(memory_space=pltpu.VMEM)
    anywhere = pl.BlockSpec(memory_space=pl.ANY)
    loads = feats // min(1024, feats)
    dma = pltpu.SemaphoreType.DMA
    return pl.pallas_call(
        functools.partial(
            kernel, n=n, per_row=per_row, rows=rows, width=width, chunk=chunk, tile=tile,
            count=float(v * total), bound=200.0 / paths_total),
        in_specs=[vm, anywhere, vm, vm, vm, anywhere],
        out_specs=[anywhere, vm],
        out_shape=[jax.ShapeDtypeStruct((v, feats), F32), jax.ShapeDtypeStruct((v, cols), F32)],
        scratch_shapes=[
            pltpu.VMEM((k, feats), jnp.int32),
            pltpu.VMEM((v, feats), F32),
            pltpu.VMEM((cols, k), BF),
            pltpu.VMEM((cols, feats), BF),
            pltpu.VMEM((feats, cols), BF),
            pltpu.VMEM((cols, feats), F8),
            pltpu.VMEM((1, feats), F32),
            pltpu.VMEM((1, feats), F32),
            pltpu.VMEM((v, feats), F32),
            pltpu.VMEM((2, v, feats), F32),
            pltpu.VMEM((v, feats), F32),
            pltpu.VMEM((v, feats), F32),
            pltpu.VMEM((2 * v, feats), BF),
            pltpu.VMEM((2 * v, feats), F8),
            pltpu.VMEM((2 * v, cols), BF),
            pltpu.VMEM((2 * v, cols), F8),
            pltpu.VMEM((v, cols), F32),
            pltpu.VMEM((n, rows, width), F32),
            pltpu.VMEM((rows, width), F32),
            pltpu.VMEM((rows, width), F32),
            pltpu.VMEM((rows, width), F32),
            pltpu.VMEM((v, cols), F32),
            pltpu.VMEM((8, 128), F32),
            pltpu.VMEM((n, 8, 128), F32),
            dma((pieces_of,)), dma((2, pieces_of)),
            dma((n,)), dma((n,)), dma((n,)), dma((n,)), dma((n,)), dma((n,)),
            dma((loads,)), dma((loads,)), dma,
        ],
        compiler_params=pltpu.CompilerParams(
            collective_id=0, has_side_effects=True, vmem_limit_bytes=60 << 20),
        name="fit",
    )(factors, frequency, phases, amplitude, targets, coeffs)


def solution(mesh):
    n = mesh.shape["feats"]

    def body(factors, frequency, phases, amplitude, targets, coeffs_init):
        total = frequency.shape[1] * n
        paths_total = factors.shape[0] * mesh.shape["paths"]
        return results(*fit(
            factors, frequency, phases[None, :], amplitude[None, :], targets, coeffs_init, n, total, paths_total))

    return jax.shard_map(
        body,
        mesh=mesh,
        in_specs=(
            P(("groups", "paths"), None),
            P(None, "feats"),
            P("feats"),
            P("feats"),
            P(None, ("groups", "paths")),
            P(None, ("groups", "feats")),
        ),
        out_specs=(P(None, ("groups", "feats")), P(None, ("groups", "paths"))),
        check_vma=False,
    )
```

```python
import functools
import math

import jax
import jax.numpy as jnp
from jax import lax
from jax.experimental import pallas as pl
from jax.experimental.pallas import tpu as pltpu
from jax.sharding import PartitionSpec as P

huber_cap = 1.0
step_rate = 0.2
momentum = 0.9
epsilon = 1e-06
ITERS = 3
BF = jnp.bfloat16
F8 = jnp.float8_e4m3fn
F32 = jnp.float32
MESH = pl.DeviceIdType.MESH
NT = (((1,), (1,)), ((), ()))

TURN = 0.0025 / (2.0 * math.pi)
C0, C1, C2, C3 = -0.7991282213187093, 3.943309301080472, -3.236024302046346, -0.3193029597879815
COS_GAIN = 3.131803039470962
LO_GAIN = 2.0**17
CLIP_GAIN = 256.0
INIT_GAIN = 64.0
DIGIT = 16.0


def cos_turns(t):
    r = t - jnp.round(t)
    u = r * r
    y = ((u + C2) * u + C1) * u + C0
    return y * y + C3


def split(x):
    hi = x.astype(BF)
    return hi, (x - hi.astype(F32)).astype(BF)


def digits(x):
    first = x.astype(F8)
    return first, ((x - first.astype(F32)) * DIGIT).astype(F8)


def joined(small, v):
    return small[:v] + small[v:] * (1.0 / DIGIT)


def kernel(
    fac_ref, freq_ref, phase_ref, amp_ref, target_ref, init_ref, coef_out, pred_ref,
    freq_buf, coef, wave, fac, hi, turned, lo, gain, rel, mine, pair, grad, velocity, ys, y8, xs, x8, image, pieces, state, track, out, sent,
    sq_mine, sq_all,
    pair_send, pair_recv, rs_send, rs_recv, ag_send, ag_recv, sq_send, sq_recv, freq_sem, init_sem, coef_sem,
    *, n, per_row, rows, width, chunk, tile, count, bound,
):
    v, cols = image.shape
    feats = mine.shape[1]
    per_chunk = chunk // width
    chunks = cols // chunk
    groups = n // per_row
    core = lax.axis_index("paths")
    me = lax.axis_index("feats")
    other = 1 - core

    btile = min(1024, feats)
    loads = feats // btile

    def load_copies(j):
        at = pl.ds(pl.multiple_of(j * btile, btile), btile)
        return (
            pltpu.make_async_copy(freq_ref.at[:, at], freq_buf.at[:, at], freq_sem.at[j]),
            pltpu.make_async_copy(init_ref.at[:, at], coef.at[:, at], init_sem.at[j]))

    for j in range(loads):
        for copy in load_copies(j):
            copy.start()

    barrier = pltpu.get_barrier_semaphore()
    pl.semaphore_signal(barrier, inc=1, device_id={"paths": other}, device_id_type=MESH)
    for d in range(1, n):
        pl.semaphore_signal(barrier, inc=1, device_id={"feats": lax.rem(me + d, n)}, device_id_type=MESH)

    def spot(j):
        r = pl.ds(pl.multiple_of((j // per_row) * rows, rows), rows)
        c = pl.ds(pl.multiple_of(lax.rem(j, per_row) * width, width), width)
        return r, c

    def columns(j, size):
        return pl.ds(pl.multiple_of(j * size, size), size)

    def pair_copy(slot, j, size):
        at = columns(j, size)
        return pltpu.make_async_remote_copy(
            mine.at[:, at], pair.at[slot, :, at], pair_send.at[j], pair_recv.at[slot, j],
            device_id={"paths": other}, device_id_type=MESH)

    def rs_copy(j):
        return pltpu.make_async_remote_copy(
            image.at[spot(j)], pieces.at[me], rs_send.at[j], rs_recv.at[me],
            device_id={"feats": j}, device_id_type=MESH)

    def rs_arrival(s):
        return pltpu.make_async_remote_copy(
            image.at[spot(me)], pieces.at[s], rs_send.at[s], rs_recv.at[s],
            device_id={"feats": s}, device_id_type=MESH)

    def ag_copy(j):
        return pltpu.make_async_remote_copy(
            out, sent.at[spot(me)], ag_send.at[j], ag_recv.at[me],
            device_id={"feats": j}, device_id_type=MESH)

    def ag_arrival(s):
        return pltpu.make_async_remote_copy(
            out, sent.at[spot(s)], ag_send.at[s], ag_recv.at[s],
            device_id={"feats": s}, device_id_type=MESH)

    def sq_copy(j):
        return pltpu.make_async_remote_copy(
            sq_mine, sq_all.at[me], sq_send.at[j], sq_recv.at[me],
            device_id={"feats": j}, device_id_type=MESH)

    def sq_arrival(s):
        return pltpu.make_async_remote_copy(
            sq_mine, sq_all.at[s], sq_send.at[s], sq_recv.at[s],
            device_id={"feats": s}, device_id_type=MESH)

    amp = amp_ref[...]
    top = jnp.max(amp, axis=1, keepdims=True)
    gain[...] = amp * COS_GAIN
    rel[...] = amp / top
    k = fac_ref.shape[1]
    fac[:, :k] = fac_ref[...].astype(F32).astype(BF)
    fac[:, k:] = jnp.ones((fac.shape[0], k), BF)
    wave[k:, :] = jnp.zeros((k, wave.shape[1]), BF)
    velocity[...] = jnp.zeros_like(velocity)
    track[...] = jnp.zeros_like(track)

    def build(j, carry):
        at = columns(j, btile)
        for copy in load_copies(j):
            copy.wait()
        wave[:k, :] = freq_buf[:, at].astype(F32).astype(BF)
        phase = phase_ref[:, at].astype(F32) * (1.0 / (1024.0 * TURN))
        first, rest = split(phase)
        third = phase - first.astype(F32) - rest.astype(F32)
        row = lax.broadcasted_iota(jnp.int32, (16, btile), 0)
        parts = jnp.where(row == 0, first.astype(F32), jnp.where(row == 1, rest.astype(F32), jnp.where(row == 2, third, 0.0)))
        wave[k : k + 16, :] = parts.astype(BF)
        c = cos_turns(jnp.dot(fac[...], wave[...], preferred_element_type=F32) * TURN)
        h = c.astype(BF)
        hi[:, at] = h
        turned[at, :] = h.T
        lo[:, at] = ((c - h.astype(F32)) * LO_GAIN).astype(F8)
        w = coef[:, at]
        ys[:v, at], ys[v:, at] = split(w * gain[:, at])
        y8[:v, at], y8[v:, at] = digits(w * rel[:, at] * INIT_GAIN)
        return carry

    lax.fori_loop(0, loads, build, 0)
    pl.semaphore_wait(barrier, n)

    def push(lo_scale):
        own = lax.rem(me, per_row) // per_chunk
        if chunks == 4:
            order = [3 - own, lax.rem(own + 2, 4), own + 1 - 2 * lax.rem(own, 2), own]
        else:
            order = [lax.rem(own + 1 + i, chunks) for i in range(chunks)]
        for c in order:
            at = columns(c, chunk)
            big = jnp.dot(ys[...], turned[:, at], preferred_element_type=F32)
            small = lax.dot_general(y8[...], lo[at, :], NT, preferred_element_type=F32)
            image[:, at] = big[:v] + big[v:] + joined(small, v) * lo_scale
            for g in range(groups):
                for e in range(per_chunk):
                    j = g * per_row + c * per_chunk + e

                    @pl.when(j != me)
                    def _():
                        rs_copy(j).start()

    def reduced():
        total = image[spot(me)]
        for d in range(1, n):
            s = lax.rem(me + d, n)
            rs_arrival(s).wait_recv()
            total = total + pieces[s]
        return total

    def mirrored(d):
        if n & (n - 1):
            return lax.rem(me + d, n)
        j, bit = me, 1
        while bit < n:
            if d & bit:
                j = j + bit - 2 * bit * lax.rem(me // bit, 2)
            bit *= 2
        return j

    def spread(value):
        out[...] = value
        for d in range(1, n):
            ag_copy(mirrored(d)).start()
        sent[spot(me)] = value

    halves = per_row // 2
    side = lax.rem(me, per_row) // halves
    near, far = columns(side, cols // 2), columns(1 - side, cols // 2)

    def settled():
        for d in range(1, n):
            rs_copy(lax.rem(me + d, n)).wait_send()

    def gathered(late):
        for d in range(1, n):
            if late == bool(d & halves and not n & (n - 1)):
                ag_arrival(mirrored(d)).wait_recv()

    def all_spread():
        for d in range(1, n):
            ag_copy(lax.rem(me + d, n)).wait_send()

    push(top * (COS_GAIN / (INIT_GAIN * LO_GAIN)))
    start = reduced()
    state[...] = start
    spread(jnp.clip(start - target_ref[spot(me)], -huber_cap, huber_cap))
    settled()

    coef_copy = pltpu.make_async_copy(coef, coef_out, coef_sem)
    top_gain = bound
    pieces_of = feats // tile

    def turn(it, carry):
        slot = lax.rem(it, 2)
        def arrange(part):
            x = sent[:, part]
            xs[:v, part], xs[v:, part] = split(x)
            x8[:v, part], x8[v:, part] = digits(x * CLIP_GAIN)

        def pulled(part, at):
            big = jnp.dot(xs[:, part], hi[part, at], preferred_element_type=F32)
            small = jnp.dot(x8[:, part], lo[part, at], preferred_element_type=F32)
            return big[:v] + big[v:] + joined(small, v) * (1.0 / (CLIP_GAIN * LO_GAIN))

        gathered(False)
        arrange(near)
        for j in range(pieces_of):
            at = columns(j, tile)
            mine[:, at] = pulled(near, at)
        gathered(True)
        arrange(far)
        for j in range(pieces_of):
            at = columns(j, tile)
            mine[:, at] = mine[:, at] + pulled(far, at)
            pair_copy(slot, j, tile).start()

        def join(j, squares):
            at = columns(j, tile)
            pair_copy(slot, j, tile).wait()
            u = mine[:, at] + pair[slot, :, at]
            g = u * gain[:, at]
            grad[:, at] = g
            ys[:v, at], ys[v:, at] = split(g * gain[:, at])
            r = rel[:, at]
            y8[:v, at], y8[v:, at] = digits(u * (r * r) * top_gain)
            square = g * g
            fold = sum(square[k : k + 8] for k in range(0, v, 8))
            return squares + sum(fold[:, k : k + 128] for k in range(0, tile, 128))

        squares = lax.fori_loop(0, pieces_of, join, jnp.zeros((8, 128), F32))
        sq_mine[...] = squares
        for d in range(1, n):
            sq_copy(lax.rem(me + d, n)).start()
        sq_all[me] = squares

        push(top * top * (COS_GAIN * COS_GAIN / (top_gain * LO_GAIN)))

        all_spread()
        for d in range(1, n):
            sq_arrival(lax.rem(me + d, n)).wait_recv()
        squares = jnp.sum(sq_all[...], axis=0)
        squares = jnp.sum(jnp.sum(squares, axis=0, keepdims=True), axis=1, keepdims=True)
        scale = jnp.sqrt(squares / count + epsilon)

        moved = momentum * track[...] + reduced() / scale
        track[...] = moved
        predicted = state[...] - step_rate * moved
        state[...] = predicted
        clipped = jnp.clip(predicted - target_ref[spot(me)], -huber_cap, huber_cap)
        spread(jnp.where(it == ITERS - 1, predicted, clipped))

        def advance(j, carry):
            at = columns(j, tile)
            vel = momentum * velocity[:, at] + grad[:, at] / scale
            velocity[:, at] = vel
            coef[:, at] = coef[:, at] - step_rate * vel
            return carry

        lax.fori_loop(0, pieces_of, advance, 0)
        for d in range(1, n):
            sq_copy(lax.rem(me + d, n)).wait_send()

        @pl.when(it == ITERS - 1)
        def _():
            coef_copy.start()

        settled()
        return carry

    lax.fori_loop(0, ITERS, turn, 0)
    gathered(False)
    gathered(True)
    pred_ref[...] = sent[...]
    all_spread()
    coef_copy.wait()


def result_kernel(coef_ref, pred_ref, coef_out, pred_out, coef, pred, in_sem, out_sem):
    steps = [(pred_ref, pred, pred_out)]
    for r in range(0, coef.shape[0], 8):
        steps.append((coef_ref.at[r : r + 8], coef.at[r : r + 8], coef_out.at[r : r + 8]))
    loads = [pltpu.make_async_copy(a, b, in_sem.at[i]) for i, (a, b, _) in enumerate(steps)]
    stores = [pltpu.make_async_copy(b, c, out_sem.at[i]) for i, (_, b, c) in enumerate(steps)]
    for load in loads:
        load.start()
    for load, store in zip(loads, stores):
        load.wait()
        store.start()
    for store in stores:
        store.wait()


def results(coeffs, predicted):
    anywhere = pl.BlockSpec(memory_space=pl.ANY)
    steps = 1 + coeffs.shape[0] // 8
    return pl.pallas_call(
        result_kernel,
        in_specs=[anywhere, anywhere],
        out_specs=[anywhere, anywhere],
        out_shape=[jax.ShapeDtypeStruct(x.shape, x.dtype) for x in (coeffs, predicted)],
        scratch_shapes=[
            pltpu.VMEM(coeffs.shape, F32),
            pltpu.VMEM(predicted.shape, F32),
            pltpu.SemaphoreType.DMA((steps,)),
            pltpu.SemaphoreType.DMA((steps,)),
        ],
        name="results",
    )(coeffs, predicted)


def fit(factors, frequency, phases, amplitude, targets, coeffs, n, total, paths_total):
    cols, k = factors.shape
    v, feats = coeffs.shape
    per_row = min(n, cols // 128)
    width = cols // per_row
    rows = v // (n // per_row)
    chunk = max(width, min(256, cols))
    tile = min(2048, feats)
    pieces_of = feats // tile
    vm = pl.BlockSpec(memory_space=pltpu.VMEM)
    anywhere = pl.BlockSpec(memory_space=pl.ANY)
    loads = feats // min(1024, feats)
    dma = pltpu.SemaphoreType.DMA
    return pl.pallas_call(
        functools.partial(
            kernel, n=n, per_row=per_row, rows=rows, width=width, chunk=chunk, tile=tile,
            count=float(v * total), bound=200.0 / paths_total),
        in_specs=[vm, anywhere, vm, vm, vm, anywhere],
        out_specs=[anywhere, vm],
        out_shape=[jax.ShapeDtypeStruct((v, feats), F32), jax.ShapeDtypeStruct((v, cols), F32)],
        scratch_shapes=[
            pltpu.VMEM((k, feats), jnp.int32),
            pltpu.VMEM((v, feats), F32),
            pltpu.VMEM((2 * k, feats // loads), BF),
            pltpu.VMEM((cols, 2 * k), BF),
            pltpu.VMEM((cols, feats), BF),
            pltpu.VMEM((feats, cols), BF),
            pltpu.VMEM((cols, feats), F8),
            pltpu.VMEM((1, feats), F32),
            pltpu.VMEM((1, feats), F32),
            pltpu.VMEM((v, feats), F32),
            pltpu.VMEM((2, v, feats), F32),
            pltpu.VMEM((v, feats), F32),
            pltpu.VMEM((v, feats), F32),
            pltpu.VMEM((2 * v, feats), BF),
            pltpu.VMEM((2 * v, feats), F8),
            pltpu.VMEM((2 * v, cols), BF),
            pltpu.VMEM((2 * v, cols), F8),
            pltpu.VMEM((v, cols), F32),
            pltpu.VMEM((n, rows, width), F32),
            pltpu.VMEM((rows, width), F32),
            pltpu.VMEM((rows, width), F32),
            pltpu.VMEM((rows, width), F32),
            pltpu.VMEM((v, cols), F32),
            pltpu.VMEM((8, 128), F32),
            pltpu.VMEM((n, 8, 128), F32),
            dma((pieces_of,)), dma((2, pieces_of)),
            dma((n,)), dma((n,)), dma((n,)), dma((n,)), dma((n,)), dma((n,)),
            dma((loads,)), dma((loads,)), dma,
        ],
        compiler_params=pltpu.CompilerParams(
            collective_id=0, has_side_effects=True, vmem_limit_bytes=60 << 20),
        name="fit",
    )(factors, frequency, phases, amplitude, targets, coeffs)


def solution(mesh):
    n = mesh.shape["feats"]

    def body(factors, frequency, phases, amplitude, targets, coeffs_init):
        total = frequency.shape[1] * n
        paths_total = factors.shape[0] * mesh.shape["paths"]
        return results(*fit(
            factors, frequency, phases[None, :], amplitude[None, :], targets, coeffs_init, n, total, paths_total))

    return jax.shard_map(
        body,
        mesh=mesh,
        in_specs=(
            P(("groups", "paths"), None),
            P(None, "feats"),
            P("feats"),
            P("feats"),
            P(None, ("groups", "paths")),
            P(None, ("groups", "feats")),
        ),
        out_specs=(P(None, ("groups", "feats")), P(None, ("groups", "paths"))),
        check_vma=False,
    )
```
